32 devices in a mesh: section: 2 (over core), row: 4 (over z), col: 4 (over y, x).
Axes of the slice: x: 2, y: 2, z: 4, core: 2. Of those that a mesh axis runs over, the one named last changes fastest.
Arguments:
- queries: bfloat16 [16384, 4096], P(('section', 'col'), 'row'), may hold values from -8 to 8
- keys: bfloat16 [16384, 512], P(('section', 'col')), may hold values from -6 to 6
- values: bfloat16 [16384, 512], P(('section', 'col')), may hold values from -6 to 6
- out_grad: bfloat16 [16384, 4096], P(('section', 'col'), 'row'), may hold values from -12 to 12
- q_weight: bfloat16 [2048, 4096], P('col', 'row'), may hold values from -0.125 to 0.125
- k_weight: bfloat16 [2048, 512], P('col'), may hold values from -0.125 to 0.125
- v_weight: bfloat16 [2048, 512], P('col'), may hold values from -0.125 to 0.125
- resid_grad: bfloat16 [16384, 2048], P(('section', 'row', 'col')), may hold values from -4 to 4
- moe_input: bfloat16 [16384, 2048], P(('section', 'row', 'col')), may hold values from -6 to 6
- expert_ids: int32 [16384, 8], P(('section', 'row', 'col')), may hold values from 0 to 31, all different within a row; in each aligned block of 512 rows (0 to 511, 512 to 1023, ...) at most 144 rows name the same one
- route_weights: float32 [16384, 8], P(('section', 'row', 'col')), may hold values from 0.03 to 0.4
- w_gate_up: bfloat16 [32, 2048, 1536], P(('section', 'row', 'col')), may hold values from -0.125 to 0.125
- w_down: bfloat16 [32, 768, 2048], P(('section', 'row', 'col')), may hold values from -0.21875 to 0.21875
Outputs:
- moe_input_grad: bfloat16 [16384, 2048], P(('section', 'row', 'col'))
The draws below stay inside these ranges and needn't reach their ends.
Inputs may be any that keep to these rules, and one draw needn't show every extreme that they name: `expert_ids`: each row names 8 different experts; among the rows of one device no expert is named by more than 144 rows, and in every draw some expert is named by exactly 144 rows of some device.
All inputs are finite; a program needn't handle non-finite values.
Results may differ from the reference program's by a relative error of at most 0.02.
Values may be sent and summed in bfloat16 or wider, within the bound.
A program may use at most 256 MiB of HBM per device.

```python
import math
import jax
import jax.numpy as jnp
import numpy as np
from jax import lax

D = 2048
HEADS = 32
KV_HEADS = 4
HEAD_DIM = 128
EXP_FF = 768
TOPK = 8
DOC = 1024
EXPERTS = 32
TOK_MOE = 512
TOKENS = 16384
HQ_DEV = 8
CAP = 144
N_ROW = 4
N_COL = 4


def draw_keys(key, part):
    shape = (TOKENS, KV_HEADS * HEAD_DIM)
    base = jnp.clip(jax.random.normal(jax.random.fold_in(key, 11), shape, jnp.float32), -6.0, 6.0)
    return base.astype(jnp.bfloat16)


def draw_queries(key, part):
    shape = (TOKENS, HEADS * HEAD_DIM)
    base = jnp.clip(jax.random.normal(jax.random.fold_in(key, 21), shape, jnp.float32), -6.0, 6.0)
    return base.astype(jnp.bfloat16)


def level_of(own_key, shape, pieces, least, high):
    factor_of, own = 1.0, jax.random.fold_in(own_key, 6)
    for dim, blocks in pieces:
        draws = jnp.exp(jax.random.uniform(jax.random.fold_in(own, dim), (blocks,), jnp.float32, least / len(pieces), high / len(pieces)))
        factor_of = factor_of * jnp.repeat(draws, shape[dim] // blocks).reshape([-1 if axis == dim else 1 for axis in range(len(shape))])
    return factor_of


def assign_block(key, own, number, rows, amount, top, most, slope):
    ranking = jax.random.permutation(key, amount)
    heavy_load, ordinary = shares(amount, rows * top, most, slope, True), shares(amount, rows * top, most, slope, False)
    places = jnp.arange(amount)

    def named(sizes, offset_by):
        used = int((sizes > 0).sum())
        fixed = max(1, used // 4)
        moved = fixed + (places - fixed + offset_by * (used - fixed)) % max(1, amount - fixed)
        return jnp.zeros((amount,), jnp.int32).at[ranking[jnp.where(places < fixed, places, moved)]].set(jnp.asarray(sizes, jnp.int32))

    sizes = jnp.where(number % 4 == 0, named(heavy_load, number // 4), named(ordinary, number - number // 4 - 1))
    mixed = jax.random.permutation(jax.random.fold_in(own, 3), amount)
    giver, sink = mixed[0:amount // 2 * 2:2], mixed[1:amount // 2 * 2:2]
    margin = jnp.minimum(sizes[giver] - 1, most - sizes[sink]) // 2
    margin = jnp.where((giver == ranking[0]) | (sink == ranking[0]) | (sizes[sink] == 0), 0, jnp.maximum(margin, 0))
    moved = jax.random.randint(jax.random.fold_in(own, 4), (amount // 2,), 0, 1 << 20) % (margin + 1)
    sizes = sizes.at[giver].add(-moved).at[sink].add(moved)
    items = jnp.searchsorted(jnp.cumsum(sizes), jnp.arange(rows * top), side="right").astype(jnp.int32)
    grid = items.reshape(top, rows).T
    grid = grid[jax.random.permutation(jax.random.fold_in(own, 1), rows)]
    offset_by = jax.random.randint(jax.random.fold_in(own, 2), (rows, 1), 0, top)
    return jnp.take_along_axis(grid, (jnp.arange(top)[None, :] + offset_by) % top, axis=1)


def shares(number_of, total, most, skew, full):
    portions = [(1 << 20) // math.isqrt(rank ** skew) + 1 for rank in range(1, number_of + 1)]
    largest = most if full else min(most, max(-(-total // number_of), total * portions[0] // sum(portions)))
    least = 1 if total - largest >= number_of - 1 else 0
    counts, spare = [largest] + [least] * (number_of - 1), total - largest - least * (number_of - 1)
    while spare > 0:
        movable = [i for i in range(1, number_of) if counts[i] < largest] or [i for i in range(1, number_of) if counts[i] < most]
        whole, left = sum([portions[i] for i in movable]), spare
        for i in movable:
            extra = min(most - counts[i], max(1, left * portions[i] // whole), spare)
            counts[i] = counts[i] + extra
            spare = spare - extra
    return np.array(counts)


def scatter_about(rng, extent, scale, most, cuts=(), held_as=jnp.bfloat16):
    values = jax.random.normal(rng, extent, jnp.float32) * scale
    if len(cuts) > 0:
        values = level_of(rng, extent, cuts, -0.22, 0.18) * values
    return jnp.clip(values, min=-most, max=most).astype(held_as)


def setup_inputs(seed: int = 0) -> dict:
    seeds = jax.random.split(jax.random.key(seed), 14)
    queries = draw_queries(jax.random.fold_in(seeds[13], 71), 0)
    keys = draw_keys(jax.random.fold_in(seeds[13], 71), 0)
    values = scatter_about(seeds[2], (TOKENS, KV_HEADS * HEAD_DIM), 1.0, 6.0, ((0, 8),))
    out_grad = scatter_about(seeds[3], (TOKENS, HEADS * HEAD_DIM), 2.0, 12.0, ((0, 8), (1, 4)))
    q_weight = scatter_about(seeds[4], (D, HEADS * HEAD_DIM), D ** -0.5, 0.125, ((0, 4), (1, 4)))
    k_weight = scatter_about(seeds[5], (D, KV_HEADS * HEAD_DIM), D ** -0.5, 0.125, ((0, 4),))
    v_weight = scatter_about(seeds[6], (D, KV_HEADS * HEAD_DIM), D ** -0.5, 0.125, ((0, 4),))
    resid_grad = scatter_about(seeds[7], (TOKENS, D), 0.5, 4.0, ((0, 32),))
    moe_input = scatter_about(seeds[8], (TOKENS, D), 1.0, 6.0, ((0, 32),))
    expert_ids_keys = jax.random.split(jax.random.fold_in(seeds[9], 1), TOKENS // TOK_MOE)
    expert_ids_turns = jax.random.permutation(jax.random.fold_in(seeds[9], 3), TOKENS // TOK_MOE)
    expert_ids = jax.vmap(lambda own, number: assign_block(jax.random.fold_in(seeds[9], 2), own, number, TOK_MOE, EXPERTS, TOPK, CAP, 2))(expert_ids_keys, expert_ids_turns).reshape((TOKENS, TOPK))
    route_weights = jnp.clip(jnp.exp(math.log(0.4) - 2.5902672 * jax.random.uniform(seeds[10], (TOKENS, TOPK), jnp.float32) ** level_of(seeds[10], (TOKENS, TOPK), ((0, 32),), -0.2, 0.2)), 0.03, 0.4)
    w_gate_up = scatter_about(seeds[11], (EXPERTS, D, 2 * EXP_FF), D ** -0.5, 0.125, ((0, 32),))
    w_down = scatter_about(seeds[12], (EXPERTS, EXP_FF, D), EXP_FF ** -0.5, 0.21875, ((0, 32),))
    return {"queries": queries, "keys": keys, "values": values, "out_grad": out_grad, "q_weight": q_weight, "k_weight": k_weight, "v_weight": v_weight, "resid_grad": resid_grad, "moe_input": moe_input, "expert_ids": expert_ids, "route_weights": route_weights, "w_gate_up": w_gate_up, "w_down": w_down}


def expert_math(rows_in, grad_in, w_gu, w_dn):
    width = w_dn.shape[0]
    gate_up = jnp.dot(rows_in, w_gu, preferred_element_type=jnp.float32)
    gate = gate_up[:, :width]
    up_part = gate_up[:, width:]
    dhidden = lax.dot_general(grad_in, w_dn, (((1,), (1,)), ((), ())), preferred_element_type=jnp.float32)
    sigm = jax.nn.sigmoid(gate)
    d_gate = dhidden * up_part * sigm * (1.0 + gate * (1.0 - sigm))
    d_up = dhidden * gate * sigm
    dgate_up = jnp.concatenate([d_gate, d_up], axis=1).astype(jnp.bfloat16)
    back_rows = lax.dot_general(dgate_up, w_gu, (((1,), (1,)), ((), ())), preferred_element_type=jnp.float32)
    return back_rows.astype(jnp.bfloat16)


def reference(queries, keys, values, out_grad, q_weight, k_weight, v_weight, resid_grad, moe_input, expert_ids, route_weights, w_gate_up, w_down):
    group_size = HEADS // KV_HEADS
    num_docs = TOKENS // DOC
    section_total = TOKENS // (N_ROW * N_COL * TOK_MOE)
    scale_val = HEAD_DIM ** -0.5
    qd = queries.reshape(num_docs, DOC, HEADS, HEAD_DIM)
    od = out_grad.reshape(num_docs, DOC, HEADS, HEAD_DIM)
    kd = keys.reshape(num_docs, DOC, KV_HEADS, HEAD_DIM)
    vd = values.reshape(num_docs, DOC, KV_HEADS, HEAD_DIM)
    kv_of_group = (jnp.arange(N_ROW) * HQ_DEV) // group_size
    wq_groups = jnp.transpose(q_weight.reshape(D, N_ROW, HQ_DEV * HEAD_DIM), (1, 0, 2))
    wk_groups = jnp.transpose(k_weight.reshape(D, KV_HEADS, HEAD_DIM)[:, kv_of_group], (1, 0, 2))
    wv_groups = jnp.transpose(v_weight.reshape(D, KV_HEADS, HEAD_DIM)[:, kv_of_group], (1, 0, 2))
    wcat_groups = jnp.concatenate([wq_groups, wk_groups, wv_groups], axis=2).astype(jnp.float32)
    causal = jnp.arange(DOC)[:, None] >= jnp.arange(DOC)[None, :]

    def one_doc(block):
        query_blk, grad_blk, key_blk, value_blk = block
        key_rep = jnp.repeat(key_blk, group_size, axis=1).astype(jnp.float32)
        value_rep = jnp.repeat(value_blk, group_size, axis=1).astype(jnp.float32)
        query_f = query_blk.astype(jnp.float32)
        grad_f = grad_blk.astype(jnp.float32)
        scores = jnp.einsum('qhd,khd->hqk', query_f, key_rep) * scale_val
        scores = jnp.where(causal[None], scores, -jnp.inf)
        top = jnp.max(scores, axis=-1, keepdims=True)
        expo = jnp.exp(scores - top)
        probs = expo / jnp.sum(expo, axis=-1, keepdims=True)
        probs_b = probs.astype(jnp.bfloat16)
        dprob = jnp.einsum('qhd,khd->hqk', grad_f, value_rep)
        delta = jnp.sum(probs * dprob, axis=-1, keepdims=True)
        dscore = (probs * (dprob - delta)).astype(jnp.bfloat16)
        dscore_f = dscore.astype(jnp.float32)
        dquery = (jnp.einsum('hqk,khd->qhd', dscore_f, key_rep) * scale_val).astype(jnp.bfloat16)
        dscore_g = dscore_f.reshape(N_ROW, HQ_DEV, DOC, DOC)
        probs_g = probs_b.astype(jnp.float32).reshape(N_ROW, HQ_DEV, DOC, DOC)
        query_g = query_f.reshape(DOC, N_ROW, HQ_DEV, HEAD_DIM)
        grad_g = grad_f.reshape(DOC, N_ROW, HQ_DEV, HEAD_DIM)
        dkey = (jnp.einsum('ghqk,qghd->gkd', dscore_g, query_g) * scale_val).astype(jnp.bfloat16)
        dvalue = jnp.einsum('ghqk,qghd->gkd', probs_g, grad_g).astype(jnp.bfloat16)
        dquery_g = jnp.transpose(dquery.reshape(DOC, N_ROW, HQ_DEV * HEAD_DIM), (1, 0, 2))
        dqkv = jnp.concatenate([dquery_g, dkey, dvalue], axis=2).astype(jnp.float32)
        part = jnp.einsum('gtc,gdc->gtd', dqkv, wcat_groups)
        part = lax.optimization_barrier(part.astype(jnp.bfloat16)).astype(jnp.float32)
        return jnp.sum(part, axis=0)

    head_grad = lax.map(one_doc, (qd, od, kd, vd))
    head_grad = head_grad.reshape(section_total, N_COL, N_ROW, TOK_MOE, D)
    head_grad = jnp.transpose(head_grad, (0, 2, 1, 3, 4)).reshape(TOKENS, D)
    layer_grad = head_grad + resid_grad.astype(jnp.float32)
    row_grad = layer_grad.astype(jnp.bfloat16)

    limit = EXPERTS * CAP
    rows_pad = jnp.concatenate([moe_input, jnp.zeros((1, D), jnp.bfloat16)], axis=0)
    grads_pad = jnp.concatenate([row_grad, jnp.zeros((1, D), jnp.bfloat16)], axis=0)

    def per_expert(carry, expert):
        hits = expert_ids == expert
        weight = jnp.sum(jnp.where(hits, route_weights, jnp.zeros_like(route_weights)), axis=1)
        weight_pad = jnp.concatenate([weight, jnp.zeros((1,), weight.dtype)], axis=0)
        chosen = jnp.any(hits, axis=1)
        index_list = jnp.nonzero(chosen, size=limit, fill_value=TOKENS)[0].astype(jnp.int32)
        result = expert_math(rows_pad[index_list], grads_pad[index_list], w_gate_up[expert], w_down[expert])
        carry = carry.at[index_list].add(weight_pad[index_list][:, None] * result.astype(jnp.float32))
        return carry, None

    start = jnp.zeros((TOKENS + 1, D), jnp.float32)
    total, unused = lax.scan(per_expert, start, jnp.arange(EXPERTS, dtype=jnp.int32))
    return total[:TOKENS].astype(jnp.bfloat16)
```

```python
from functools import partial

import jax
import jax.numpy as jnp
from jax import lax
from jax.experimental import pallas as pl
from jax.experimental.pallas import tpu as pltpu
from jax.sharding import PartitionSpec as P

HEADS = 32
KV_HEADS = 4
HEAD_DIM = 128
TOPK = 8
DOC = 1024
CHUNKS = 2


def pick_kernel(pos_ref, rows_ref, out_ref):
    cap = out_ref.shape[2]
    tokens = rows_ref.shape[1]
    pos = pos_ref[0, 0]
    slot = lax.broadcasted_iota(jnp.int32, (cap, tokens), 0)
    onehot = jnp.where(slot == pos, 1.0, 0.0).astype(jnp.bfloat16)
    picked = jnp.dot(onehot, rows_ref[0], preferred_element_type=jnp.float32)
    out_ref[0, 0] = picked.astype(out_ref.dtype)


def pick_rows(pos, rows, cap):
    peers, groups, _, tokens = pos.shape
    width = rows.shape[2]
    return pl.pallas_call(
        pick_kernel,
        grid=(groups, peers),
        in_specs=[
            pl.BlockSpec((1, 1, 1, tokens), lambda g, p: (p, g, 0, 0)),
            pl.BlockSpec((1, tokens, width), lambda g, p: (g, 0, 0)),
        ],
        out_specs=pl.BlockSpec((1, 1, cap, width), lambda g, p: (p, g, 0, 0)),
        out_shape=jax.ShapeDtypeStruct((peers, groups, cap, width), rows.dtype),
        cost_estimate=pl.CostEstimate(
            flops=2 * peers * groups * cap * tokens * width,
            bytes_accessed=2 * width * groups * (tokens + peers * cap),
            transcendentals=0,
        ),
        name="pick_rows",
    )(pos, rows)


def mix_kernel(pos_ref, weight_ref, rows_ref, out_ref, total_ref):
    peer = pl.program_id(1)
    cap = rows_ref.shape[2]
    tokens = out_ref.shape[0]
    slot = lax.broadcasted_iota(jnp.int32, (cap, tokens), 0)
    spread = jnp.where(slot == pos_ref[0, 0], weight_ref[0, 0], 0.0).astype(jnp.bfloat16)
    term = lax.dot_general(
        spread, rows_ref[0, 0], (((0,), (0,)), ((), ())), preferred_element_type=jnp.float32
    )

    @pl.when(peer == 0)
    def _():
        total_ref[...] = term

    @pl.when(peer > 0)
    def _():
        total_ref[...] += term

    @pl.when(peer == pl.num_programs(1) - 1)
    def _():
        out_ref[...] = total_ref[...].astype(out_ref.dtype)


def mix_rows(pos, weight, rows):
    peers, groups, _, tokens = pos.shape
    cap, width = rows.shape[2:]
    return pl.pallas_call(
        mix_kernel,
        grid=(groups, peers),
        in_specs=[
            pl.BlockSpec((1, 1, 1, tokens), lambda g, p: (p, g, 0, 0)),
            pl.BlockSpec((1, 1, 1, tokens), lambda g, p: (p, g, 0, 0)),
            pl.BlockSpec((1, 1, cap, width), lambda g, p: (p, g, 0, 0)),
        ],
        out_specs=pl.BlockSpec((tokens, width), lambda g, p: (g, 0)),
        out_shape=jax.ShapeDtypeStruct((groups * tokens, width), rows.dtype),
        scratch_shapes=[pltpu.VMEM((tokens, width), jnp.float32)],
        cost_estimate=pl.CostEstimate(
            flops=2 * peers * groups * cap * tokens * width,
            bytes_accessed=2 * width * groups * (tokens + peers * cap),
            transcendentals=0,
        ),
        name="mix_rows",
    )(pos, weight, rows)


def doc_backward(block, scale_val):
    query_blk, grad_blk, key_blk, value_blk = block
    doc_len = query_blk.shape[0]
    heads_here = query_blk.shape[1]
    causal = jnp.arange(doc_len)[:, None] >= jnp.arange(doc_len)[None, :]
    scores = (
        jnp.einsum("qhd,kd->hqk", query_blk, key_blk, preferred_element_type=jnp.float32)
        * scale_val
    )
    scores = jnp.where(causal[None], scores, -jnp.inf)
    top = jnp.max(scores, axis=-1, keepdims=True)
    expo = jnp.exp(scores - top)
    probs = expo / jnp.sum(expo, axis=-1, keepdims=True)
    probs_b = probs.astype(jnp.bfloat16)
    dprob = jnp.einsum("qhd,kd->hqk", grad_blk, value_blk, preferred_element_type=jnp.float32)
    delta = jnp.sum(probs * dprob, axis=-1, keepdims=True)
    dscore = (probs * (dprob - delta)).astype(jnp.bfloat16)
    dquery = (
        jnp.einsum("hqk,kd->qhd", dscore, key_blk, preferred_element_type=jnp.float32) * scale_val
    ).astype(jnp.bfloat16)
    dkey = (
        jnp.einsum("hqk,qhd->kd", dscore, query_blk, preferred_element_type=jnp.float32) * scale_val
    ).astype(jnp.bfloat16)
    dvalue = jnp.einsum(
        "hqk,qhd->kd", probs_b, grad_blk, preferred_element_type=jnp.float32
    ).astype(jnp.bfloat16)
    return jnp.concatenate(
        [dquery.reshape(doc_len, heads_here * key_blk.shape[1]), dkey, dvalue], axis=1
    )


def body(
    queries,
    keys,
    values,
    out_grad,
    q_weight,
    k_weight,
    v_weight,
    resid_grad,
    moe_input,
    expert_ids,
    route_weights,
    w_gate_up,
    w_down,
):
    row_count = lax.axis_size("row")
    heads_here = queries.shape[1] // HEAD_DIM
    group_size = HEADS // KV_HEADS
    kv_index = lax.axis_index("row") * heads_here // group_size
    key_head = lax.dynamic_slice_in_dim(keys, kv_index * HEAD_DIM, HEAD_DIM, 1)
    value_head = lax.dynamic_slice_in_dim(values, kv_index * HEAD_DIM, HEAD_DIM, 1)
    wk_local = lax.dynamic_slice_in_dim(k_weight, kv_index * HEAD_DIM, HEAD_DIM, 1)
    wv_local = lax.dynamic_slice_in_dim(v_weight, kv_index * HEAD_DIM, HEAD_DIM, 1)
    wcat_local = jnp.concatenate([q_weight, wk_local, wv_local], axis=1)
    wcat_whole = lax.all_gather(wcat_local, "col", axis=0, tiled=True)
    section_count = lax.axis_size("section")
    col_count = lax.axis_size("col")
    peers = section_count * col_count
    n_experts = peers * row_count
    tok_rows = queries.shape[0]
    moe_rows = tok_rows // row_count
    model = q_weight.shape[0] * col_count
    capacity = max(2, 9 * moe_rows * TOPK // (8 * n_experts))

    ids_line = lax.all_gather(expert_ids, "row", axis=0, tiled=False)
    weights_line = lax.all_gather(route_weights, "row", axis=0, tiled=False)
    rows_line = lax.all_gather(moe_input, "row", axis=0, tiled=False)
    peer = jnp.arange(peers, dtype=jnp.int32)
    peer_expert = (
        (peer // col_count) * row_count + lax.axis_index("row")
    ) * col_count + peer % col_count
    named = ids_line[None] == peer_expert[:, None, None, None]
    hit = jnp.any(named, axis=-1)
    weight = jnp.sum(jnp.where(named, weights_line[None], 0.0), axis=-1)
    order = jnp.arange(moe_rows, dtype=jnp.int32)
    before = (order[:, None] < order[None, :]).astype(jnp.bfloat16)
    rank = lax.dot_general(
        hit.astype(jnp.bfloat16).reshape(peers * row_count, moe_rows),
        before,
        (((1,), (0,)), ((), ())),
        preferred_element_type=jnp.float32,
    ).reshape(peers, row_count, moe_rows)
    pos = jnp.where(hit, rank.astype(jnp.int32), -1)[:, :, None, :]
    weight = weight[:, :, None, :]

    def swap(blocks):
        return lax.all_to_all(
            blocks, ("section", "col"), split_axis=0, concat_axis=0, tiled=True
        )

    w_gu = w_gate_up[0]
    w_dn = w_down[0]
    ff = w_dn.shape[0]
    rows_in = swap(pick_rows(pos, rows_line, capacity)).reshape(-1, model)
    gate_up = jnp.dot(rows_in, w_gu, preferred_element_type=jnp.float32)

    doc_count = tok_rows // DOC
    query_docs = queries.reshape(doc_count, DOC, heads_here, HEAD_DIM)
    grad_docs = out_grad.reshape(doc_count, DOC, heads_here, HEAD_DIM)
    key_docs = key_head.reshape(doc_count, DOC, HEAD_DIM)
    value_docs = value_head.reshape(doc_count, DOC, HEAD_DIM)
    dqkv = lax.map(
        partial(doc_backward, scale_val=HEAD_DIM ** (-0.5)),
        (query_docs, grad_docs, key_docs, value_docs),
    )
    dqkv = dqkv.reshape(tok_rows, dqkv.shape[-1])

    span = model // CHUNKS
    dhidden = None
    for chunk in range(CHUNKS):
        lo, hi = chunk * span, (chunk + 1) * span
        term = lax.dot_general(
            dqkv,
            wcat_whole[lo:hi],
            (((1,), (1,)), ((), ())),
            preferred_element_type=jnp.float32,
        )
        head_grad = lax.psum_scatter(
            term.astype(jnp.bfloat16), "row", scatter_dimension=0, tiled=True
        ).astype(jnp.float32)
        layer_grad = head_grad + resid_grad[:, lo:hi].astype(jnp.float32)
        row_grad = layer_grad.astype(jnp.bfloat16)
        grads_line = lax.all_gather(row_grad, "row", axis=0, tiled=False)
        grads_in = swap(pick_rows(pos, grads_line, capacity)).reshape(-1, span)
        piece = lax.dot_general(
            grads_in,
            w_dn[:, lo:hi],
            (((1,), (1,)), ((), ())),
            preferred_element_type=jnp.float32,
        )
        dhidden = piece if dhidden is None else dhidden + piece

    gate = gate_up[:, :ff]
    up_part = gate_up[:, ff:]
    sigm = jax.nn.sigmoid(gate)
    d_gate = dhidden * up_part * sigm * (1.0 + gate * (1.0 - sigm))
    d_up = dhidden * gate * sigm
    dgate_up = jnp.concatenate([d_gate, d_up], axis=1).astype(jnp.bfloat16)

    pieces = []
    for chunk in range(CHUNKS):
        lo, hi = chunk * span, (chunk + 1) * span
        back_rows = lax.dot_general(
            dgate_up,
            w_gu[lo:hi],
            (((1,), (1,)), ((), ())),
            preferred_element_type=jnp.float32,
        ).astype(jnp.bfloat16)
        returned = swap(back_rows.reshape(peers, row_count, capacity, span))
        mixed = mix_rows(pos, weight, returned)
        pieces.append(lax.psum_scatter(mixed, "row", scatter_dimension=0, tiled=True))
    return jnp.concatenate(pieces, axis=1)


def solution(mesh):
    return jax.shard_map(
        body,
        mesh=mesh,
        in_specs=(
            P(("section", "col"), "row"),
            P(("section", "col"), None),
            P(("section", "col"), None),
            P(("section", "col"), "row"),
            P("col", "row"),
            P("col", None),
            P("col", None),
            P(("section", "row", "col"), None),
            P(("section", "row", "col"), None),
            P(("section", "row", "col"), None),
            P(("section", "row", "col"), None),
            P(("section", "row", "col"), None, None),
            P(("section", "row", "col"), None, None),
        ),
        out_specs=P(("section", "row", "col"), None),
        check_vma=False,
    )
```

```python
import jax
import jax.numpy as jnp
from jax import lax
from jax.experimental import pallas as pl
from jax.experimental.pallas import tpu as pltpu
from jax.sharding import PartitionSpec as P

HEADS = 32
KV_HEADS = 4
HEAD_DIM = 128
TOPK = 8
DOC = 1024
CHUNKS = 4
PART = 512
ATT_BLOCK = 256
LOG2_E = 1.4426950408889634


def slot_hits(pos, cap):
    slot = lax.broadcasted_iota(jnp.int32, (cap, pos.shape[1]), 0)
    return slot == pos


def pick_kernel(pos_ref, rows_ref, out_ref):
    peers, _, cap, width = out_ref.shape
    picks = [
        jnp.where(slot_hits(pos_ref[p, 0], cap), 1.0, 0.0).astype(jnp.bfloat16)
        for p in range(peers)
    ]
    if cap % 16 == 0:
        picked = jnp.dot(
            jnp.concatenate(picks, axis=0), rows_ref[0], preferred_element_type=jnp.float32
        ).astype(out_ref.dtype)
        out_ref[:, 0] = picked.reshape(peers, cap, width)
    else:
        for p in range(peers):
            picked = jnp.dot(picks[p], rows_ref[0], preferred_element_type=jnp.float32)
            out_ref[p, 0] = picked.astype(out_ref.dtype)


def pick_rows(pos, rows, cap):
    peers, groups, _, tokens = pos.shape
    width = rows.shape[2]
    part = min(PART, width)
    return pl.pallas_call(
        pick_kernel,
        grid=(groups, width // part),
        in_specs=[
            pl.BlockSpec((peers, 1, 1, tokens), lambda g, w: (0, g, 0, 0)),
            pl.BlockSpec((1, tokens, part), lambda g, w: (g, 0, w)),
        ],
        out_specs=pl.BlockSpec((peers, 1, cap, part), lambda g, w: (0, g, 0, w)),
        out_shape=jax.ShapeDtypeStruct((peers, groups, cap, width), rows.dtype),
        cost_estimate=pl.CostEstimate(
            flops=2 * peers * groups * cap * tokens * width,
            bytes_accessed=2 * width * groups * (tokens + peers * cap),
            transcendentals=0,
        ),
        name="pick_rows",
    )(pos, rows)


def mix_kernel(pos_ref, weight_ref, rows_ref, out_ref):
    peers, _, cap, width = rows_ref.shape
    spreads = [
        jnp.where(slot_hits(pos_ref[p, 0], cap), weight_ref[p, 0], 0.0).astype(jnp.bfloat16)
        for p in range(peers)
    ]
    across = (((0,), (0,)), ((), ()))
    if cap % 16 == 0:
        total = lax.dot_general(
            jnp.concatenate(spreads, axis=0),
            rows_ref[:, 0].reshape(peers * cap, width),
            across,
            preferred_element_type=jnp.float32,
        )
    else:
        total = jnp.zeros(out_ref.shape, jnp.float32)
        for p in range(peers):
            total += lax.dot_general(
                spreads[p], rows_ref[p, 0], across, preferred_element_type=jnp.float32
            )
    out_ref[...] = total.astype(out_ref.dtype)


def mix_rows(pos, weight, rows):
    peers, groups, _, tokens = pos.shape
    cap, width = rows.shape[2:]
    part = min(PART, width)
    return pl.pallas_call(
        mix_kernel,
        grid=(groups, width // part),
        in_specs=[
            pl.BlockSpec((peers, 1, 1, tokens), lambda g, w: (0, g, 0, 0)),
            pl.BlockSpec((peers, 1, 1, tokens), lambda g, w: (0, g, 0, 0)),
            pl.BlockSpec((peers, 1, cap, part), lambda g, w: (0, g, 0, w)),
        ],
        out_specs=pl.BlockSpec((tokens, part), lambda g, w: (g, w)),
        out_shape=jax.ShapeDtypeStruct((groups * tokens, width), rows.dtype),
        cost_estimate=pl.CostEstimate(
            flops=2 * peers * groups * cap * tokens * width,
            bytes_accessed=2 * width * groups * (tokens + peers * cap),
            transcendentals=0,
        ),
        name="mix_rows",
    )(pos, weight, rows)


def doc_kernel(query_ref, grad_ref, key_ref, value_ref, out_ref, dkey_ref, dvalue_ref):
    head = pl.program_id(1)
    doc_len, dim = query_ref.shape
    scale_val = dim ** (-0.5)
    block = min(ATT_BLOCK, doc_len)

    @pl.when(head == 0)
    def _():
        dkey_ref[...] = jnp.zeros_like(dkey_ref)
        dvalue_ref[...] = jnp.zeros_like(dvalue_ref)

    key_turned = key_ref[...].T
    columns = pl.ds(pl.multiple_of(head * dim, dim), dim)
    for at in range(0, doc_len, block):
        seen = at + block
        query = query_ref[at:seen, :]
        grad = grad_ref[at:seen, :]
        scores = lax.dot_general(
            key_ref[:seen, :],
            query,
            (((1,), (1,)), ((), ())),
            preferred_element_type=jnp.float32,
        )
        key_at = lax.broadcasted_iota(jnp.int32, (block, block), 0)
        query_at = lax.broadcasted_iota(jnp.int32, (block, block), 1)
        corner = jnp.where(key_at <= query_at, scores[at:, :], -jnp.inf)
        scores = jnp.concatenate([scores[:at, :], corner], axis=0) if at else corner
        top = jnp.max(scores, axis=0, keepdims=True)
        expo = jnp.exp2((scores - top) * (scale_val * LOG2_E))
        probs = expo * (1.0 / jnp.sum(expo, axis=0, keepdims=True))
        dprob = lax.dot_general(
            value_ref[:seen, :],
            grad,
            (((1,), (1,)), ((), ())),
            preferred_element_type=jnp.float32,
        )
        delta = jnp.sum(probs * dprob, axis=0, keepdims=True)
        dscore = (probs * (dprob - delta)).astype(jnp.bfloat16)
        dvalue_ref[:seen, :] += jnp.dot(
            probs.astype(jnp.bfloat16), grad, preferred_element_type=jnp.float32
        )
        dkey_ref[:seen, :] += jnp.dot(dscore, query, preferred_element_type=jnp.float32)
        turned = jnp.dot(key_turned[:, :seen], dscore, preferred_element_type=jnp.float32)
        out_ref[at:seen, columns] = (turned.T * scale_val).astype(out_ref.dtype)

    @pl.when(head == pl.num_programs(1) - 1)
    def _():
        heads = out_ref.shape[1] // dim - 2
        out_ref[:, heads * dim : (heads + 1) * dim] = (dkey_ref[...] * scale_val).astype(
            out_ref.dtype
        )
        out_ref[:, (heads + 1) * dim :] = dvalue_ref[...].astype(out_ref.dtype)


def attention_backward(queries, out_grad, key_head, value_head):
    rows, width = queries.shape
    dim = key_head.shape[1]
    docs, heads = rows // DOC, width // dim
    return pl.pallas_call(
        doc_kernel,
        grid=(docs, heads),
        in_specs=[
            pl.BlockSpec((DOC, dim), lambda d, h: (d, h)),
            pl.BlockSpec((DOC, dim), lambda d, h: (d, h)),
            pl.BlockSpec((DOC, dim), lambda d, h: (d, 0)),
            pl.BlockSpec((DOC, dim), lambda d, h: (d, 0)),
        ],
        out_specs=pl.BlockSpec((DOC, width + 2 * dim), lambda d, h: (d, 0)),
        out_shape=jax.ShapeDtypeStruct((rows, width + 2 * dim), queries.dtype),
        scratch_shapes=[pltpu.VMEM((DOC, dim), jnp.float32)] * 2,
        cost_estimate=pl.CostEstimate(
            flops=10 * docs * heads * DOC * DOC * dim,
            bytes_accessed=2 * rows * (3 * width + 4 * dim),
            transcendentals=docs * heads * DOC * DOC,
        ),
        name="doc_backward",
    )(queries, out_grad, key_head, value_head)


def body(
    queries,
    keys,
    values,
    out_grad,
    q_weight,
    k_weight,
    v_weight,
    resid_grad,
    moe_input,
    expert_ids,
    route_weights,
    w_gate_up,
    w_down,
):
    row_count = lax.axis_size("row")
    heads_here = queries.shape[1] // HEAD_DIM
    group_size = HEADS // KV_HEADS
    kv_index = lax.axis_index("row") * heads_here // group_size
    key_head = lax.dynamic_slice_in_dim(keys, kv_index * HEAD_DIM, HEAD_DIM, 1)
    value_head = lax.dynamic_slice_in_dim(values, kv_index * HEAD_DIM, HEAD_DIM, 1)
    wk_local = lax.dynamic_slice_in_dim(k_weight, kv_index * HEAD_DIM, HEAD_DIM, 1)
    wv_local = lax.dynamic_slice_in_dim(v_weight, kv_index * HEAD_DIM, HEAD_DIM, 1)
    wcat_local = jnp.concatenate([q_weight, wk_local, wv_local], axis=1)
    wcat_whole = lax.all_gather(wcat_local, "col", axis=0, tiled=True)
    section_count = lax.axis_size("section")
    col_count = lax.axis_size("col")
    peers = section_count * col_count
    n_experts = peers * row_count
    tok_rows = queries.shape[0]
    moe_rows = tok_rows // row_count
    model = q_weight.shape[0] * col_count
    capacity = max(2, 9 * moe_rows * TOPK // (8 * n_experts))

    routes = jnp.concatenate([expert_ids.astype(jnp.float32), route_weights], axis=1)
    routes_line = lax.all_gather(routes, "row", axis=0, tiled=False)
    routes_line, moe_input = lax.optimization_barrier((routes_line, moe_input))
    ids_line = routes_line[..., :TOPK].astype(jnp.int32)
    weights_line = routes_line[..., TOPK:]
    rows_line = lax.all_to_all(
        jnp.broadcast_to(moe_input[None], (row_count,) + moe_input.shape),
        "row",
        split_axis=0,
        concat_axis=0,
        tiled=True,
    )
    peer = jnp.arange(peers, dtype=jnp.int32)
    peer_expert = (
        (peer // col_count) * row_count + lax.axis_index("row")
    ) * col_count + peer % col_count
    named = ids_line[None] == peer_expert[:, None, None, None]
    hit = jnp.any(named, axis=-1)
    weight = jnp.sum(jnp.where(named, weights_line[None], 0.0), axis=-1)
    order = jnp.arange(moe_rows, dtype=jnp.int32)
    before = (order[:, None] < order[None, :]).astype(jnp.bfloat16)
    rank = lax.dot_general(
        hit.astype(jnp.bfloat16).reshape(peers * row_count, moe_rows),
        before,
        (((1,), (0,)), ((), ())),
        preferred_element_type=jnp.float32,
    ).reshape(peers, row_count, moe_rows)
    pos = jnp.where(hit, rank.astype(jnp.int32), -1)[:, :, None, :]
    weight = weight[:, :, None, :]

    def swap(blocks):
        return lax.all_to_all(
            blocks, ("section", "col"), split_axis=0, concat_axis=0, tiled=True
        )

    w_gu = w_gate_up[0]
    w_dn = w_down[0]
    ff = w_dn.shape[0]
    rows_in = swap(pick_rows(pos, rows_line, capacity)).reshape(-1, model)
    gate_up = jnp.dot(rows_in, w_gu, preferred_element_type=jnp.float32)

    dqkv = attention_backward(queries, out_grad, key_head, value_head)

    span = model // CHUNKS
    dhidden = None
    for chunk in range(CHUNKS):
        lo, hi = chunk * span, (chunk + 1) * span
        term = lax.dot_general(
            dqkv,
            wcat_whole[lo:hi],
            (((1,), (1,)), ((), ())),
            preferred_element_type=jnp.float32,
        )
        head_grad = lax.psum_scatter(
            term.astype(jnp.bfloat16), "row", scatter_dimension=0, tiled=True
        ).astype(jnp.float32)
        layer_grad = head_grad + resid_grad[:, lo:hi].astype(jnp.float32)
        row_grad = layer_grad.astype(jnp.bfloat16)
        grads_line = lax.all_gather(row_grad, "row", axis=0, tiled=False)
        grads_in = swap(pick_rows(pos, grads_line, capacity)).reshape(-1, span)
        piece = lax.dot_general(
            grads_in,
            w_dn[:, lo:hi],
            (((1,), (1,)), ((), ())),
            preferred_element_type=jnp.float32,
        )
        dhidden = piece if dhidden is None else dhidden + piece

    gate = gate_up[:, :ff]
    up_part = gate_up[:, ff:]
    sigm = jax.nn.sigmoid(gate)
    d_gate = dhidden * up_part * sigm * (1.0 + gate * (1.0 - sigm))
    d_up = dhidden * gate * sigm
    dgate_up = jnp.concatenate([d_gate, d_up], axis=1).astype(jnp.bfloat16)

    pieces = []
    for chunk in range(CHUNKS):
        lo, hi = chunk * span, (chunk + 1) * span
        back_rows = lax.dot_general(
            dgate_up,
            w_gu[lo:hi],
            (((1,), (1,)), ((), ())),
            preferred_element_type=jnp.float32,
        ).astype(jnp.bfloat16)
        returned = swap(back_rows.reshape(peers, row_count, capacity, span))
        mixed = mix_rows(pos, weight, returned)
        pieces.append(lax.psum_scatter(mixed, "row", scatter_dimension=0, tiled=True))
    return jnp.concatenate(pieces, axis=1)


def solution(mesh):
    return jax.shard_map(
        body,
        mesh=mesh,
        in_specs=(
            P(("section", "col"), "row"),
            P(("section", "col"), None),
            P(("section", "col"), None),
            P(("section", "col"), "row"),
            P("col", "row"),
            P("col", None),
            P("col", None),
            P(("section", "row", "col"), None),
            P(("section", "row", "col"), None),
            P(("section", "row", "col"), None),
            P(("section", "row", "col"), None),
            P(("section", "row", "col"), None, None),
            P(("section", "row", "col"), None, None),
        ),
        out_specs=P(("section", "row", "col"), None),
        check_vma=False,
    )
```

```python
import jax
import jax.numpy as jnp
from jax import lax
from jax.experimental import pallas as pl
from jax.experimental.pallas import tpu as pltpu
from jax.sharding import PartitionSpec as P

HEADS = 32
KV_HEADS = 4
HEAD_DIM = 128
TOPK = 8
DOC = 1024
CHUNKS = 2
PART = 512
ATT_BLOCK = 256
LOG2_E = 1.4426950408889634


def slot_hits(pos, cap):
    slot = lax.broadcasted_iota(jnp.int32, (cap, pos.shape[1]), 0)
    return slot == pos


def pick_kernel(pos_ref, rows_ref, out_ref):
    peers, _, cap, width = out_ref.shape
    picks = [
        jnp.where(slot_hits(pos_ref[p, 0], cap), 1.0, 0.0).astype(jnp.bfloat16)
        for p in range(peers)
    ]
    if cap % 16 == 0:
        picked = jnp.dot(
            jnp.concatenate(picks, axis=0), rows_ref[0], preferred_element_type=jnp.float32
        ).astype(out_ref.dtype)
        out_ref[:, 0] = picked.reshape(peers, cap, width)
    else:
        for p in range(peers):
            picked = jnp.dot(picks[p], rows_ref[0], preferred_element_type=jnp.float32)
            out_ref[p, 0] = picked.astype(out_ref.dtype)


def pick_rows(pos, rows, cap):
    peers, groups, _, tokens = pos.shape
    width = rows.shape[2]
    part = min(PART, width)
    return pl.pallas_call(
        pick_kernel,
        grid=(groups, width // part),
        in_specs=[
            pl.BlockSpec((peers, 1, 1, tokens), lambda g, w: (0, g, 0, 0)),
            pl.BlockSpec((1, tokens, part), lambda g, w: (g, 0, w)),
        ],
        out_specs=pl.BlockSpec((peers, 1, cap, part), lambda g, w: (0, g, 0, w)),
        out_shape=jax.ShapeDtypeStruct((peers, groups, cap, width), rows.dtype),
        cost_estimate=pl.CostEstimate(
            flops=2 * peers * groups * cap * tokens * width,
            bytes_accessed=2 * width * groups * (tokens + peers * cap),
            transcendentals=0,
        ),
        name="pick_rows",
    )(pos, rows)


def mix_kernel(pos_ref, weight_ref, rows_ref, out_ref):
    peers, _, cap, width = rows_ref.shape
    spreads = [
        jnp.where(slot_hits(pos_ref[p, 0], cap), weight_ref[p, 0], 0.0).astype(jnp.bfloat16)
        for p in range(peers)
    ]
    across = (((0,), (0,)), ((), ()))
    if cap % 16 == 0:
        total = lax.dot_general(
            jnp.concatenate(spreads, axis=0),
            rows_ref[:, 0].reshape(peers * cap, width),
            across,
            preferred_element_type=jnp.float32,
        )
    else:
        total = jnp.zeros(out_ref.shape, jnp.float32)
        for p in range(peers):
            total += lax.dot_general(
                spreads[p], rows_ref[p, 0], across, preferred_element_type=jnp.float32
            )
    out_ref[...] = total.astype(out_ref.dtype)


def mix_rows(pos, weight, rows):
    peers, groups, _, tokens = pos.shape
    cap, width = rows.shape[2:]
    part = min(PART, width)
    return pl.pallas_call(
        mix_kernel,
        grid=(groups, width // part),
        in_specs=[
            pl.BlockSpec((peers, 1, 1, tokens), lambda g, w: (0, g, 0, 0)),
            pl.BlockSpec((peers, 1, 1, tokens), lambda g, w: (0, g, 0, 0)),
            pl.BlockSpec((peers, 1, cap, part), lambda g, w: (0, g, 0, w)),
        ],
        out_specs=pl.BlockSpec((tokens, part), lambda g, w: (g, w)),
        out_shape=jax.ShapeDtypeStruct((groups * tokens, width), rows.dtype),
        cost_estimate=pl.CostEstimate(
            flops=2 * peers * groups * cap * tokens * width,
            bytes_accessed=2 * width * groups * (tokens + peers * cap),
            transcendentals=0,
        ),
        name="mix_rows",
    )(pos, weight, rows)


def doc_kernel(query_ref, grad_ref, key_ref, value_ref, out_ref, dkey_ref, dvalue_ref):
    head = pl.program_id(1)
    doc_len, dim = query_ref.shape
    scale_val = dim ** (-0.5)
    block = min(ATT_BLOCK, doc_len)

    @pl.when(head == 0)
    def _():
        dkey_ref[...] = jnp.zeros_like(dkey_ref)
        dvalue_ref[...] = jnp.zeros_like(dvalue_ref)

    key_turned = key_ref[...].T
    columns = pl.ds(pl.multiple_of(head * dim, dim), dim)
    for at in range(0, doc_len, block):
        seen = at + block
        query = query_ref[at:seen, :]
        grad = grad_ref[at:seen, :]
        scores = lax.dot_general(
            key_ref[:seen, :],
            query,
            (((1,), (1,)), ((), ())),
            preferred_element_type=jnp.float32,
        )
        key_at = lax.broadcasted_iota(jnp.int32, (block, block), 0)
        query_at = lax.broadcasted_iota(jnp.int32, (block, block), 1)
        corner = jnp.where(key_at <= query_at, scores[at:, :], -jnp.inf)
        scores = jnp.concatenate([scores[:at, :], corner], axis=0) if at else corner
        top = jnp.max(scores, axis=0, keepdims=True)
        expo = jnp.exp2((scores - top) * (scale_val * LOG2_E))
        probs = expo * (1.0 / jnp.sum(expo, axis=0, keepdims=True))
        dprob = lax.dot_general(
            value_ref[:seen, :],
            grad,
            (((1,), (1,)), ((), ())),
            preferred_element_type=jnp.float32,
        )
        delta = jnp.sum(probs * dprob, axis=0, keepdims=True)
        dscore = (probs * (dprob - delta)).astype(jnp.bfloat16)
        dvalue_ref[:seen, :] += jnp.dot(
            probs.astype(jnp.bfloat16), grad, preferred_element_type=jnp.float32
        )
        dkey_ref[:seen, :] += jnp.dot(dscore, query, preferred_element_type=jnp.float32)
        turned = jnp.dot(key_turned[:, :seen], dscore, preferred_element_type=jnp.float32)
        out_ref[at:seen, columns] = (turned.T * scale_val).astype(out_ref.dtype)

    @pl.when(head == pl.num_programs(1) - 1)
    def _():
        heads = out_ref.shape[1] // dim - 2
        out_ref[:, heads * dim : (heads + 1) * dim] = (dkey_ref[...] * scale_val).astype(
            out_ref.dtype
        )
        out_ref[:, (heads + 1) * dim :] = dvalue_ref[...].astype(out_ref.dtype)


def attention_backward(queries, out_grad, key_head, value_head):
    rows, width = queries.shape
    dim = key_head.shape[1]
    docs, heads = rows // DOC, width // dim
    return pl.pallas_call(
        doc_kernel,
        grid=(docs, heads),
        in_specs=[
            pl.BlockSpec((DOC, dim), lambda d, h: (d, h)),
            pl.BlockSpec((DOC, dim), lambda d, h: (d, h)),
            pl.BlockSpec((DOC, dim), lambda d, h: (d, 0)),
            pl.BlockSpec((DOC, dim), lambda d, h: (d, 0)),
        ],
        out_specs=pl.BlockSpec((DOC, width + 2 * dim), lambda d, h: (d, 0)),
        out_shape=jax.ShapeDtypeStruct((rows, width + 2 * dim), queries.dtype),
        scratch_shapes=[pltpu.VMEM((DOC, dim), jnp.float32)] * 2,
        cost_estimate=pl.CostEstimate(
            flops=10 * docs * heads * DOC * DOC * dim,
            bytes_accessed=2 * rows * (3 * width + 4 * dim),
            transcendentals=docs * heads * DOC * DOC,
        ),
        name="doc_backward",
    )(queries, out_grad, key_head, value_head)


def body(
    queries,
    keys,
    values,
    out_grad,
    q_weight,
    k_weight,
    v_weight,
    resid_grad,
    moe_input,
    expert_ids,
    route_weights,
    w_gate_up,
    w_down,
):
    row_count = lax.axis_size("row")
    heads_here = queries.shape[1] // HEAD_DIM
    group_size = HEADS // KV_HEADS
    kv_index = lax.axis_index("row") * heads_here // group_size
    key_head = lax.dynamic_slice_in_dim(keys, kv_index * HEAD_DIM, HEAD_DIM, 1)
    value_head = lax.dynamic_slice_in_dim(values, kv_index * HEAD_DIM, HEAD_DIM, 1)
    wk_local = lax.dynamic_slice_in_dim(k_weight, kv_index * HEAD_DIM, HEAD_DIM, 1)
    wv_local = lax.dynamic_slice_in_dim(v_weight, kv_index * HEAD_DIM, HEAD_DIM, 1)
    wcat_local = jnp.concatenate([q_weight, wk_local, wv_local], axis=1)
    wcat_whole = lax.all_gather(wcat_local, "col", axis=0, tiled=True)
    section_count = lax.axis_size("section")
    col_count = lax.axis_size("col")
    peers = section_count * col_count
    n_experts = peers * row_count
    tok_rows = queries.shape[0]
    moe_rows = tok_rows // row_count
    model = q_weight.shape[0] * col_count
    capacity = max(2, 9 * moe_rows * TOPK // (8 * n_experts))

    routes = jnp.concatenate([expert_ids.astype(jnp.float32), route_weights], axis=1)
    routes_line = lax.all_gather(routes, "row", axis=0, tiled=False)
    routes_line, moe_input, queries = lax.optimization_barrier((routes_line, moe_input, queries))
    ids_line = routes_line[..., :TOPK].astype(jnp.int32)
    weights_line = routes_line[..., TOPK:]
    rows_line = lax.all_to_all(
        jnp.broadcast_to(moe_input[None], (row_count,) + moe_input.shape),
        "row",
        split_axis=0,
        concat_axis=0,
        tiled=True,
    )
    peer = jnp.arange(peers, dtype=jnp.int32)
    peer_expert = (
        (peer // col_count) * row_count + lax.axis_index("row")
    ) * col_count + peer % col_count
    named = ids_line[None] == peer_expert[:, None, None, None]
    hit = jnp.any(named, axis=-1)
    weight = jnp.sum(jnp.where(named, weights_line[None], 0.0), axis=-1)
    order = jnp.arange(moe_rows, dtype=jnp.int32)
    before = (order[:, None] < order[None, :]).astype(jnp.bfloat16)
    rank = lax.dot_general(
        hit.astype(jnp.bfloat16).reshape(peers * row_count, moe_rows),
        before,
        (((1,), (0,)), ((), ())),
        preferred_element_type=jnp.float32,
    ).reshape(peers, row_count, moe_rows)
    pos = jnp.where(hit, rank.astype(jnp.int32), -1)[:, :, None, :]
    weight = weight[:, :, None, :]

    def swap(blocks):
        return lax.all_to_all(
            blocks, ("section", "col"), split_axis=0, concat_axis=0, tiled=True
        )

    w_gu = w_gate_up[0]
    w_dn = w_down[0]
    ff = w_dn.shape[0]
    rows_in = swap(pick_rows(pos, rows_line, capacity))
    rows_in, pos_grads = lax.optimization_barrier((rows_in, pos))
    rows_in = rows_in.reshape(-1, model)
    gate_up = jnp.dot(rows_in, w_gu, preferred_element_type=jnp.float32)

    dqkv = attention_backward(queries, out_grad, key_head, value_head)

    span = model // CHUNKS
    dhidden = None
    for chunk in range(CHUNKS):
        lo, hi = chunk * span, (chunk + 1) * span
        term = lax.dot_general(
            dqkv,
            wcat_whole[lo:hi],
            (((1,), (1,)), ((), ())),
            preferred_element_type=jnp.float32,
        )
        head_grad = lax.psum_scatter(
            term.astype(jnp.bfloat16), "row", scatter_dimension=0, tiled=True
        ).astype(jnp.float32)
        layer_grad = head_grad + resid_grad[:, lo:hi].astype(jnp.float32)
        row_grad = layer_grad.astype(jnp.bfloat16)
        grads_line = lax.all_gather(row_grad, "row", axis=0, tiled=False)
        grads_in = swap(pick_rows(pos_grads, grads_line, capacity)).reshape(-1, span)
        piece = lax.dot_general(
            grads_in,
            w_dn[:, lo:hi],
            (((1,), (1,)), ((), ())),
            preferred_element_type=jnp.float32,
        )
        dhidden = piece if dhidden is None else dhidden + piece

    gate = gate_up[:, :ff]
    up_part = gate_up[:, ff:]
    sigm = jax.nn.sigmoid(gate)
    d_gate = dhidden * up_part * sigm * (1.0 + gate * (1.0 - sigm))
    d_up = dhidden * gate * sigm
    dgate_up = jnp.concatenate([d_gate, d_up], axis=1).astype(jnp.bfloat16)

    pieces = []
    for chunk in range(CHUNKS):
        lo, hi = chunk * span, (chunk + 1) * span
        back_rows = lax.dot_general(
            dgate_up,
            w_gu[lo:hi],
            (((1,), (1,)), ((), ())),
            preferred_element_type=jnp.float32,
        ).astype(jnp.bfloat16)
        returned = swap(back_rows.reshape(peers, row_count, capacity, span))
        mixed = mix_rows(pos, weight, returned)
        pieces.append(lax.psum_scatter(mixed, "row", scatter_dimension=0, tiled=True))
    return jnp.concatenate(pieces, axis=1)


def solution(mesh):
    return jax.shard_map(
        body,
        mesh=mesh,
        in_specs=(
            P(("section", "col"), "row"),
            P(("section", "col"), None),
            P(("section", "col"), None),
            P(("section", "col"), "row"),
            P("col", "row"),
            P("col", None),
            P("col", None),
            P(("section", "row", "col"), None),
            P(("section", "row", "col"), None),
            P(("section", "row", "col"), None),
            P(("section", "row", "col"), None),
            P(("section", "row", "col"), None, None),
            P(("section", "row", "col"), None, None),
        ),
        out_specs=P(("section", "row", "col"), None),
        check_vma=False,
    )
```
